32 devices in a mesh: src: 8 (over z, x), tgt: 4 (over y, core).
Axes of the slice: x: 2, y: 2, z: 4, core: 2. Of those that a mesh axis runs over, the one named last changes fastest.
Arguments:
- source_words: bfloat16 [4096, 300], P(('src', 'tgt')), may hold values from -3 to 3
- target_words: bfloat16 [3840, 300], P(('tgt', 'src')), may hold values from -24 to 24
Outputs:
- rotated: bfloat16 [4096, 300], P(('src', 'tgt'))
- matched: float32 [4096, 300], P(('src', 'tgt'))
- ortho: float32 [300, 300], replicated
- row_pot: float32 [4096], P(('src', 'tgt'))
- col_pot: float32 [3840], P(('tgt', 'src'))
The draws below stay inside these ranges and needn't reach their ends.
All inputs are finite; a program needn't handle non-finite values.
Results may differ from the reference program's by a relative error of at most 0.0034.
Values may be sent and summed in bfloat16 or wider, within the bound.
No kernel may reach another device: no remote copies, remote signals or barrier semaphores. Data moves between devices by JAX's collectives and lax.ppermute only.
A program may use at most 64 MiB of HBM per device.

```python
import math
import jax
import jax.numpy as jnp
from jax import lax

D = 300
ITERS = 2
NEWTON = 12
NS = 4096
NT = 3840


def source_rows(key):
    base = jax.random.normal(jax.random.fold_in(key, 11), (NS, D), jnp.float32)
    ramp = jnp.exp(jnp.linspace(math.log(0.25), math.log(4.0), NS, dtype=jnp.float32))
    return jnp.clip(base * ramp[:, None], -3.0, 3.0)


def draw_source_words(key, part):
    return source_rows(key).astype(jnp.bfloat16)


def draw_target_words(key, part):
    base = jnp.clip(jax.random.normal(jax.random.fold_in(key, 23), (NT, D), jnp.float32), -3.0, 3.0)
    return base.astype(jnp.bfloat16)


def setup_inputs(seed: int = 0) -> dict:
    key_of = jax.random.split(jax.random.key(seed), 3)
    return {
        "source_words": draw_source_words(jax.random.fold_in(key_of[2], 71), 0),
        "target_words": draw_target_words(jax.random.fold_in(key_of[2], 71), 0),
    }


def row_lse(logits):
    top = lax.optimization_barrier(jnp.max(logits, axis=1))
    return top + jnp.log(lax.optimization_barrier(jnp.sum(jnp.exp(logits - top[:, None]), axis=1)))

def reference(source_words, target_words):
    scale = 4.0 / math.sqrt(D)
    block = math.gcd(NS, 512)
    count = NS // block
    blocks = source_words.reshape(count, block, D)
    highest = lax.Precision.HIGHEST

    def scores(rows_in):
        return jnp.dot(rows_in, target_words.T, preferred_element_type=jnp.float32) * scale
    col_pot = jnp.zeros((NT,), jnp.float32)
    row_pot = jnp.zeros((NS,), jnp.float32)
    for sweep_index in range(ITERS):

        def row_block(rows_in):
            return -row_lse(scores(rows_in) + col_pot[None, :])
        row_pot = lax.map(row_block, blocks).reshape(NS)
        potentials = row_pot.reshape(count, block)

        def col_step(carry, item):
            rows_in, shift = item
            logits = scores(rows_in) + shift[:, None]
            top, total = carry
            higher = jnp.maximum(top, lax.optimization_barrier(jnp.max(logits, axis=0)))
            total = total * jnp.exp(top - higher) + lax.optimization_barrier(jnp.sum(jnp.exp(logits - higher[None, :]), axis=0))
            return ((higher, total), None)
        start = (jnp.full((NT,), -jnp.inf, jnp.float32), jnp.zeros((NT,), jnp.float32))
        (top, total), unused = lax.scan(col_step, start, (blocks, potentials))
        col_pot = -(top + jnp.log(total))
    potentials = row_pot.reshape(count, block)

    def plan_rows(item):
        rows_in, shift = item
        plan = jnp.exp(scores(rows_in) + shift[:, None] + col_pot[None, :]).astype(jnp.bfloat16)
        return jnp.dot(plan, target_words, preferred_element_type=jnp.float32)
    matched = lax.map(plan_rows, (blocks, potentials)).reshape(NS, D)
    source_full = source_words.astype(jnp.float32)
    cov = jnp.dot(source_full.T, matched, precision=highest)
    ortho = cov / jnp.sqrt(jnp.sum(cov * cov) + 1e-06)
    for step_index in range(NEWTON):
        ortho = 1.5 * ortho - 0.5 * jnp.dot(ortho, jnp.dot(ortho.T, ortho, precision=highest), precision=highest)
    rotated = jnp.dot(source_full, ortho, precision=highest).astype(jnp.bfloat16)
    return (rotated, matched, ortho, row_pot, col_pot)
```

```python
import functools
import math

import jax
import jax.numpy as jnp
from jax import lax
from jax.experimental import pallas as pl
from jax.experimental.pallas import tpu as pltpu
from jax.sharding import PartitionSpec as P

ITERS = 2
NEWTON = 12
LANES = 128
STRIP = 128
TINY = 1e-20
EMPTY = -1e30
F32 = jnp.float32
BF16 = jnp.bfloat16
NT = (((1,), (1,)), ((), ()))
TN = (((0,), (0,)), ((), ()))


ANY = pl.BlockSpec(memory_space=pl.ANY)
VMEM = pl.BlockSpec(memory_space=pltpu.VMEM)


def log_add(a, b):
    top = jnp.maximum(a, b)
    return top + jnp.log(jnp.exp(a - top) + jnp.exp(b - top))


def eye():
    rows = lax.broadcasted_iota(jnp.int32, (LANES, LANES), 0)
    return rows == lax.broadcasted_iota(jnp.int32, (LANES, LANES), 1)


def to_lanes(column):
    return jnp.sum(jnp.where(eye(), column, 0.0), axis=0, keepdims=True)


def to_column(row):
    return jnp.sum(jnp.where(eye(), row, 0.0), axis=1, keepdims=True)


def strips(rows, step):
    def one(index, carry):
        return step(pl.ds(pl.multiple_of(index * STRIP, STRIP), STRIP), carry)

    return one, rows // STRIP


def row_chunks(cols):
    return [pl.ds(c * LANES, LANES) for c in range(cols // LANES)]


def column_sums(plan_ref, weight_of, rows, cols):
    chunks = row_chunks(cols)

    def step(strip, accs):
        weight = weight_of(strip)
        out = []
        for acc, chunk in zip(accs, chunks):
            part = plan_ref[strip, chunk] * weight
            out.append(acc + jnp.sum(part.reshape(STRIP // 8, 8, LANES), axis=0))
        return tuple(out)

    one, count = strips(rows, step)
    accs = lax.fori_loop(
        0, count, one, tuple(jnp.zeros((8, LANES), F32) for _ in chunks)
    )
    return jnp.concatenate([jnp.sum(a, axis=0, keepdims=True) for a in accs], axis=1)


def first_kernel(n_src, n_tgt, lo_bits, plan, scale, block_s, block_t, *refs):
    pieces, refs = refs[: len(plan)], refs[len(plan) :]
    s_ref, t_ref, a_ref, lse_ref, s_rows, sems, row_tmp = refs
    me_s, me_t = lax.axis_index("src"), lax.axis_index("tgt")
    groups = n_tgt // 2
    copies = []
    for piece, blocks in zip(pieces, plan):
        for index, (kind, source, target) in enumerate(blocks):
            source = me_s ^ pick(source, me_t)
            target = me_t ^ target
            if kind == "s":
                slot = (source >> lo_bits) * groups + (target >> 1)
                place = s_ref.at[:, pl.ds(pl.multiple_of(slot * block_s, block_s), block_s)]
            else:
                slot = (target & 1) * n_src + source
                place = t_ref.at[:, pl.ds(pl.multiple_of(slot * LANES, LANES), LANES)]
            copies.append(pltpu.make_async_copy(piece.at[index], place, sems.at[len(copies)]))
    for copy in copies:
        copy.start()
    for copy in copies:
        copy.wait()
    rows, cols = s_rows.shape[0], t_ref.shape[1]
    s_rows[...] = s_ref[...].T
    chunks = row_chunks(cols)
    wide = 4 * LANES
    bias = jnp.where(real_columns(wide, block_t), 0.0, EMPTY)
    for start in range(0, cols, wide):
        a_ref[:, start : start + wide] = bias + jnp.dot(
            s_rows[...], t_ref[:, start : start + wide], preferred_element_type=F32
        )
    factor = scale * math.log2(math.e)

    def step(strip, carry):
        top = a_ref[strip, chunks[0]]
        for chunk in chunks[1:]:
            top = jnp.maximum(top, a_ref[strip, chunk])
        top = jnp.max(top, axis=1, keepdims=True)
        total = jnp.zeros((STRIP, LANES), F32)
        for chunk in chunks:
            part = jnp.exp2((a_ref[strip, chunk] - top) * factor)
            a_ref[strip, chunk] = part
            total = total + part
        top = top * scale
        a_ref[strip, pl.ds(cols, LANES)] = jnp.broadcast_to(top, (STRIP, LANES))
        row_tmp[strip, :] = top + jnp.log(jnp.sum(total, axis=1, keepdims=True))
        return carry

    one, count = strips(rows, step)
    lax.fori_loop(0, count, one, 0)
    for k in range(rows // LANES):
        part = pl.ds(k * LANES, LANES)
        lse_ref[:, part] = to_lanes(row_tmp[part, :])


def real_columns(cols, block_t):
    return lax.rem(lax.broadcasted_iota(jnp.int32, (1, cols), 1), LANES) < block_t


def pick(masks, me_t):
    even, odd = masks
    return even if even == odd else jnp.where((me_t & 1) == 0, even, odd)


def load_rows(row_ref, tmp_ref):
    for k in range(tmp_ref.shape[0] // LANES):
        part = pl.ds(k * LANES, LANES)
        tmp_ref[part, :] = to_column(row_ref[:, part])


def second_kernel(scale, block_t, s_hbm, t_hbm, a_ref, mine_ref, other_ref, pot_ref, lse_ref, tmp, s_ref, t_ref, sem):
    rows, cols = tmp.shape[0], lse_ref.shape[1]
    pot_ref[...] = -log_add(mine_ref[...], other_ref[...])
    load_rows(pot_ref, tmp)

    def weight(strip):
        return jnp.exp(a_ref[strip, pl.ds(cols, LANES)] + tmp[strip, :])

    sums = jnp.where(real_columns(cols, block_t), column_sums(a_ref, weight, rows, cols), 1.0)
    lse_ref[...] = jnp.log(sums)

    @pl.when(jnp.min(sums) < TINY)
    def _():
        load_both(s_hbm, t_hbm, s_ref, t_ref, sem)
        for start in range(0, cols, LANES):
            logits = jnp.dot(
                s_ref[...].T, t_ref[:, start : start + LANES], preferred_element_type=F32
            )
            logits = logits * scale + tmp[...]
            top = jnp.max(logits, axis=0, keepdims=True)
            total = jnp.sum(jnp.exp(logits - top), axis=0, keepdims=True)
            lse_ref[:, start : start + LANES] = jnp.where(
                real_columns(LANES, block_t), top + jnp.log(total), 0.0
            )


def load_both(s_hbm, t_hbm, s_ref, t_ref, sem):
    first = pltpu.make_async_copy(s_hbm, s_ref, sem.at[0])
    second = pltpu.make_async_copy(t_hbm, t_ref, sem.at[1])
    first.start()
    second.start()
    first.wait()
    second.wait()


def third_kernel(
    scale, block_t, s_hbm, t_hbm, a_in, pot_ref, mine_ref, other_ref, a_ref, lse_ref, cpot_ref, tmp, s_ref, t_ref, sem
):
    del a_in
    rows, cols = tmp.shape[0], mine_ref.shape[1]
    chunks = row_chunks(cols)
    cpot = -log_add(mine_ref[...], other_ref[...])
    high = jnp.max(cpot) > -math.log(TINY)

    @pl.when(high)
    def _():
        load_rows(pot_ref, tmp)
        load_both(s_hbm, t_hbm, s_ref, t_ref, sem)
        for start in range(0, cols, LANES):
            logits = jnp.dot(
                s_ref[...].T, t_ref[:, start : start + LANES], preferred_element_type=F32
            )
            part = logits * scale + tmp[...] + cpot[:, start : start + LANES]
            a_ref[:, start : start + LANES] = jnp.where(
                real_columns(LANES, block_t), jnp.exp(part), 0.0
            )
        a_ref[:, cols : cols + LANES] = jnp.broadcast_to(-tmp[...], (rows, LANES))

    lift = jnp.where(high, 0.0, cpot)
    cpot_ref[...] = cpot - lift
    weight = jnp.exp(lift)

    def step(strip, carry):
        total = jnp.zeros((STRIP, LANES), F32)
        for c, chunk in enumerate(chunks):
            total = total + a_ref[strip, chunk] * weight[:, c * LANES : (c + 1) * LANES]
        total = jnp.sum(total, axis=1, keepdims=True)
        tmp[strip, :] = a_ref[strip, pl.ds(cols, 1)] + jnp.log(total)
        return carry

    one, count = strips(rows, step)
    lax.fori_loop(0, count, one, 0)
    for k in range(rows // LANES):
        part = pl.ds(k * LANES, LANES)
        lse_ref[:, part] = to_lanes(tmp[part, :])


def fourth_kernel(n_tgt, lo_bits, block_t, a_ref, mine_ref, other_ref, pot_ref, own_ref, sum_ref, tmp):
    rows, cols, block_s = tmp.shape[0], sum_ref.shape[1], own_ref.shape[1]
    pot_ref[...] = -log_add(mine_ref[...], other_ref[...])
    slot = (lax.axis_index("src") >> lo_bits) * (n_tgt // 2) + (lax.axis_index("tgt") >> 1)
    own_ref[...] = pot_ref[:, pl.ds(pl.multiple_of(slot * block_s, block_s), block_s)]
    load_rows(pot_ref, tmp)

    def weight(strip):
        return jnp.exp(a_ref[strip, pl.ds(cols, LANES)] + tmp[strip, :])

    sums = column_sums(a_ref, weight, rows, cols)
    sum_ref[...] = jnp.where(real_columns(cols, block_t), sums, 1.0)


def split(x):
    high = x.astype(BF16)
    return high, (x - high.astype(F32)).astype(BF16)


def fifth_kernel(
    n_src, n_tgt, lo_bits, block_s, s_ref, t_ref, a_ref, pot_ref, mine_ref, other_ref, cpot_ref,
    matched_ref, cov_ref, own_ref, tmp, plan, matched, cov, col_tmp
):
    rows, cols, block_t = tmp.shape[0], mine_ref.shape[1], own_ref.shape[1]
    width, half = s_ref.shape[0], cov_ref.shape[1]
    chunks = row_chunks(cols)
    me_s, me_t = lax.axis_index("src"), lax.axis_index("tgt")
    side = me_t & 1
    load_rows(pot_ref, tmp)
    sums = mine_ref[...] + other_ref[...]
    col_tmp[...] = cpot_ref[...] - jnp.log(sums)
    slot = side * n_src + me_s
    own_ref[...] = col_tmp[:, pl.ds(pl.multiple_of(slot * LANES, LANES), LANES)][:, :block_t]
    inverse = 1.0 / sums

    def step(strip, carry):
        weight = jnp.exp(a_ref[strip, pl.ds(cols, LANES)] + tmp[strip, :])
        for c, chunk in enumerate(chunks):
            part = a_ref[strip, chunk] * weight * inverse[:, c * LANES : (c + 1) * LANES]
            plan[strip, chunk] = part.astype(BF16)
        return carry

    one, count = strips(rows, step)
    lax.fori_loop(0, count, one, 0)
    matched[...] = lax.dot_general(plan[...], t_ref[...], NT, preferred_element_type=F32)
    groups = n_tgt // 2
    base = (me_s >> lo_bits) * groups
    for group in range(groups):
        place = base + ((me_t >> 1) ^ group)
        start = pl.multiple_of(place * block_s, block_s)
        matched_ref[group] = matched[pl.ds(start, block_s), :].T
    high, low = split(matched[...])
    cov[...] = jnp.zeros(cov.shape, F32)
    cov[:width, :width] = jnp.dot(s_ref[...], high, preferred_element_type=F32) + jnp.dot(
        s_ref[...], low, preferred_element_type=F32
    )
    for k in range(2):
        cov_ref[k] = cov[pl.ds(pl.multiple_of((side ^ k) * half, 8), half), :]


MAIN = 256
TAIL = 64


def tails(high, low, other):
    return (high + pltpu.roll(other, TAIL, 1)).astype(BF16), low.astype(BF16)


def polar_kernel(s_ref, mine_ref, other_ref, ortho_ref, rotated_ref, x_ref, high, low, left, right, below, gram_high, gram_low, gram_tail):
    width, half = ortho_ref.shape[0], mine_ref.shape[0]
    rows = 2 * half
    tail = rows - MAIN
    side = lax.axis_index("tgt") & 1
    x_ref[pl.ds(pl.multiple_of(side * half, 8), half), :] = mine_ref[...]
    x_ref[pl.ds(pl.multiple_of((1 - side) * half, 8), half), :] = other_ref[...]
    cov = x_ref[...]
    x_ref[...] = cov / jnp.sqrt(jnp.sum(cov * cov) + 1e-06)
    below[...] = jnp.zeros(below.shape, BF16)

    def beside(*parts):
        return jnp.concatenate(parts, axis=1)

    def left_of(part):
        return beside(high[part, :MAIN], high[part, :MAIN], low[part, :MAIN], left[part, :])

    def right_of(part):
        return beside(high[part, :MAIN], low[part, :MAIN], high[part, :MAIN], right[part, :])

    def step(index, carry):
        x = x_ref[...]
        x_high = x.astype(BF16)
        rest = x - x_high.astype(F32)
        x_low = rest.astype(BF16)
        high[...] = x_high
        low[...] = x_low
        high_tail, low_tail = x_high[:, MAIN:].astype(F32), rest[:, MAIN:]
        left[:, :LANES], left[:, LANES:] = tails(high_tail, low_tail, high_tail)
        right[:, :LANES], right[:, LANES:] = tails(high_tail, high_tail, low_tail)
        for k, part in enumerate((x_high, x_low, x_high)):
            below[k * TAIL : k * TAIL + tail, :] = part[MAIN:]
        first, last = slice(0, MAIN), slice(MAIN, rows)
        gram = lax.dot_general(
            left_of(slice(0, rows)), right_of(first), NT, preferred_element_type=F32
        )
        corner = lax.dot_general(left_of(last), right_of(last), NT, preferred_element_type=F32)
        corner = jnp.concatenate([gram[MAIN:, :].T, corner], axis=0)
        corner = beside(corner, jnp.zeros((rows, LANES - tail), F32))
        part = gram.astype(BF16)
        gram_high[...] = part
        gram_low[...] = (gram - part.astype(F32)).astype(BF16)
        corner_high = corner.astype(BF16).astype(F32)
        gram_tail[:, :LANES], gram_tail[:, LANES:] = tails(
            corner_high, corner - corner_high, corner_high
        )
        product = jnp.dot(
            beside(gram_high[...], gram_high[...], gram_low[...], gram_tail[...]),
            jnp.concatenate(
                [high[:MAIN, :rows], low[:MAIN, :rows], high[:MAIN, :rows], below[:, :rows]], axis=0
            ),
            preferred_element_type=F32,
        )
        x_ref[:, :rows] = 1.5 * x_ref[:, :rows] - 0.5 * product
        return carry

    lax.fori_loop(0, NEWTON, step, 0)
    ortho = x_ref[:width, :width]
    ortho_ref[...] = ortho
    ortho_high, ortho_low = split(ortho)
    rotated = lax.dot_general(
        ortho_high, s_ref[...], TN, preferred_element_type=F32
    ) + lax.dot_general(ortho_low, s_ref[...], TN, preferred_element_type=F32)
    rotated_ref[...] = rotated.astype(BF16)


def log2(n):
    return n.bit_length() - 1


def make_body(n_src, n_tgt):
    groups = n_tgt // 2

    def send(x, masks):
        pairs = []
        for s in range(n_src):
            for t in range(n_tgt):
                source, target = masks[t & 1]
                pairs.append((s * n_tgt + t, (s ^ source) * n_tgt + (t ^ target)))
        return lax.ppermute(x, ("src", "tgt"), pairs)

    def shifted(blocks, masks, crossed=False):
        out = []
        for kind, source, target in blocks:
            source = source[::-1] if crossed else source
            source = tuple(a ^ m[0] for a, m in zip(source, masks))
            out.append((kind, source, target ^ masks[0][1]))
        return out

    def groups_of(parts):
        return [parts] if len(parts) < 2 else [parts[:-1], parts[-1:]]

    def send_parts(parts, masks, crossed=False):
        out = []
        for group in groups_of(parts):
            whole = jnp.concatenate([x for x, _ in group], axis=0) if len(group) > 1 else group[0][0]
            blocks = [block for _, names in group for block in names]
            out.append((send(whole, masks), shifted(blocks, masks, crossed)))
        return out

    def gather(source_t, target_t, high_src, low_src, high_tgt):
        pad = ((0, 0), (0, source_t.shape[1] - target_t.shape[1]))
        both = lax.optimization_barrier(jnp.stack([source_t, jnp.pad(target_t, pad)]))
        pairs = [(both, [("s", (0, 0), 0), ("t", (0, 0), 0)])]
        for mask in high_src[::-1]:
            masks = (mask, mask)
            pairs += [(send(x, masks), shifted(blocks, masks)) for x, blocks in pairs]
        sources = [(x[:1], blocks[:1]) for x, blocks in pairs]
        targets = [(x[1:], blocks[1:]) for x, blocks in pairs]
        parts = list(pairs)
        core = ((0, 1), (0, 1))
        parts += send_parts(targets, core, True)
        for k in range(max(len(high_tgt), len(low_src))):
            if k < len(low_src):
                more = send_parts(targets, (low_src[k], low_src[k]))
                targets = targets + more
                parts += more
                for part in more:
                    parts += send_parts([part], core, True)
            if k < len(high_tgt):
                more = send_parts(sources, (high_tgt[k], high_tgt[k]))
                sources = sources + more
                parts += more
        return [x for x, _ in parts], [blocks for _, blocks in parts]

    def meet(x, stages, combine):
        for mask in stages[:-1]:
            x = combine(x, send(x, (mask, mask)))
        return x, send(x, (stages[-1], stages[-1]))

    def body(source_words, target_words):
        block_s, width = source_words.shape
        block_t = target_words.shape[0]
        scale = 4.0 / math.sqrt(width)
        assert block_t <= LANES
        cols = LANES * n_src * 2
        rep = n_src
        while rep > 1 and block_s * rep * groups * cols * 4 > 9 * 2**20:
            rep //= 2
        rows = block_s * rep * groups
        lo_bits = log2(n_src // rep)
        bits = log2(n_src)
        low_src = [(1 << k, 0) for k in range(lo_bits)]
        high_src = [(1 << k, 0) for k in range(lo_bits, bits)]
        high_tgt = [(0, 1 << k) for k in range(1, log2(n_tgt))]
        core = [(0, 1)]
        source_t = source_words.T
        pieces, plan = gather(source_t, target_words.T, high_src, low_src, high_tgt)

        shape = jax.ShapeDtypeStruct
        a_shape = shape((rows, cols + LANES), F32)
        row_shape, col_shape = shape((1, rows), F32), shape((1, cols), F32)
        s_shape, t_shape = shape((width, rows), BF16), shape((width, cols), BF16)
        big = rows * cols * 4 > 9 * 2**20
        params = pltpu.CompilerParams(vmem_limit_bytes=(56 if big else 16) * 2**20)
        tmp = pltpu.VMEM((rows, 1), F32)
        again = [pltpu.VMEM(s_shape.shape, BF16), pltpu.VMEM(t_shape.shape, BF16), pltpu.SemaphoreType.DMA((2,))]

        s_all, t_all, block, row_lse = pl.pallas_call(
            functools.partial(first_kernel, n_src, n_tgt, lo_bits, plan, scale, block_s, block_t),
            out_shape=(s_shape, t_shape, a_shape, row_shape),
            in_specs=[ANY] * len(pieces),
            out_specs=(VMEM,) * 4,
            scratch_shapes=[
                pltpu.VMEM((rows, width), BF16),
                pltpu.SemaphoreType.DMA((rows // block_s + cols // LANES,)),
                tmp,
            ],
            compiler_params=params,
        )(*pieces)

        mine, other = meet(row_lse, high_tgt, log_add)
        row_pot, col_lse = pl.pallas_call(
            functools.partial(second_kernel, scale, block_t),
            out_shape=(row_shape, col_shape),
            in_specs=[ANY, ANY, VMEM, VMEM, VMEM],
            out_specs=(VMEM,) * 2,
            scratch_shapes=[tmp] + again,
            compiler_params=params,
        )(s_all, t_all, block, mine, other)

        mine, other = meet(col_lse, core + low_src, log_add)
        block, row_lse, col_base = pl.pallas_call(
            functools.partial(third_kernel, scale, block_t),
            out_shape=(a_shape, row_shape, col_shape),
            in_specs=[ANY, ANY, VMEM, VMEM, VMEM, VMEM],
            out_specs=(VMEM,) * 3,
            input_output_aliases={2: 0},
            scratch_shapes=[tmp] + again,
            compiler_params=params,
        )(s_all, t_all, block, row_pot, mine, other)

        mine, other = meet(row_lse, high_tgt, log_add)
        row_pot, row_part, col_sum = pl.pallas_call(
            functools.partial(fourth_kernel, n_tgt, lo_bits, block_t),
            out_shape=(row_shape, shape((1, block_s), F32), col_shape),
            in_specs=[VMEM] * 3,
            out_specs=(VMEM,) * 3,
            scratch_shapes=[tmp],
            compiler_params=params,
        )(block, mine, other)

        mine, other = meet(col_sum, core + low_src, jnp.add)
        assert 0 < width - MAIN <= TAIL
        half = (width + 15) // 16 * 8
        padded = (width + LANES - 1) // LANES * LANES
        matched, cov, col_part = pl.pallas_call(
            functools.partial(fifth_kernel, n_src, n_tgt, lo_bits, block_s),
            out_shape=(
                shape((groups, width, block_s), F32),
                shape((2, half, padded), F32),
                shape((1, block_t), F32),
            ),
            in_specs=[VMEM] * 7,
            out_specs=(VMEM,) * 3,
            scratch_shapes=[
                tmp,
                pltpu.VMEM((rows, cols), BF16),
                pltpu.VMEM((rows, width), F32),
                pltpu.VMEM((2 * half, padded), F32),
                pltpu.VMEM((1, cols), F32),
            ],
            compiler_params=params,
        )(s_all, t_all, block, row_pot, mine, other, col_base)

        part = cov[0] + send(cov[1], (core[0], core[0]))
        stages = low_src + high_tgt
        for k in range(len(stages)):
            part = part + send(part, (stages[k], stages[(k + 1) % len(stages)]))
        own_matched = matched[0]
        sent, part = lax.optimization_barrier(([matched[k] for k in range(1, groups)], part))
        rest = send(part, (core[0], core[0]))
        late = [send(x, ((0, 2 * k), (0, 2 * k))) for k, x in enumerate(sent, 1)]

        ortho, rotated = pl.pallas_call(
            polar_kernel,
            out_shape=(shape((width, width), F32), shape((width, block_s), BF16)),
            in_specs=[VMEM] * 3,
            out_specs=(VMEM,) * 2,
            scratch_shapes=[
                pltpu.VMEM((2 * half, padded), F32),
                pltpu.VMEM((2 * half, padded), BF16),
                pltpu.VMEM((2 * half, padded), BF16),
                pltpu.VMEM((2 * half, 2 * LANES), BF16),
                pltpu.VMEM((2 * half, 2 * LANES), BF16),
                pltpu.VMEM((4 * TAIL, padded), BF16),
                pltpu.VMEM((2 * half, MAIN), BF16),
                pltpu.VMEM((2 * half, MAIN), BF16),
                pltpu.VMEM((2 * half, 2 * LANES), BF16),
            ],
            compiler_params=params,
        )(source_t, part, rest)
        own_matched, rotated = lax.optimization_barrier((own_matched, rotated))
        for theirs in late:
            own_matched = own_matched + theirs
        return (rotated.T, own_matched.T, ortho, row_part[0], col_part[0])

    return body


def solution(mesh):
    in_specs = (P(("src", "tgt"), None), P(("tgt", "src"), None))
    out_specs = (
        P(("src", "tgt"), None),
        P(("src", "tgt"), None),
        P(),
        P(("src", "tgt")),
        P(("tgt", "src")),
    )
    body = make_body(mesh.shape["src"], mesh.shape["tgt"])
    return jax.shard_map(body, mesh=mesh, in_specs=in_specs, out_specs=out_specs, check_vma=False)
```

```python
import functools
import math

import jax
import jax.numpy as jnp
from jax import lax
from jax.experimental import pallas as pl
from jax.experimental.pallas import tpu as pltpu
from jax.sharding import PartitionSpec as P

ITERS = 2
NEWTON = 12
LANES = 128
STRIP = 128
TINY = 1e-20
EMPTY = -1e30
F32 = jnp.float32
BF16 = jnp.bfloat16
NT = (((1,), (1,)), ((), ()))
TN = (((0,), (0,)), ((), ()))


ANY = pl.BlockSpec(memory_space=pl.ANY)
VMEM = pl.BlockSpec(memory_space=pltpu.VMEM)


def log_add(a, b):
    top = jnp.maximum(a, b)
    return top + jnp.log(jnp.exp(a - top) + jnp.exp(b - top))


def eye():
    rows = lax.broadcasted_iota(jnp.int32, (LANES, LANES), 0)
    return rows == lax.broadcasted_iota(jnp.int32, (LANES, LANES), 1)


def to_lanes(column):
    return jnp.sum(jnp.where(eye(), column, 0.0), axis=0, keepdims=True)


def to_column(row):
    return jnp.sum(jnp.where(eye(), row, 0.0), axis=1, keepdims=True)


def strips(rows, step):
    def one(index, carry):
        return step(pl.ds(pl.multiple_of(index * STRIP, STRIP), STRIP), carry)

    return one, rows // STRIP


def row_chunks(cols):
    return [pl.ds(c * LANES, LANES) for c in range(cols // LANES)]


def column_sums(plan_ref, weight_of, rows, cols):
    chunks = row_chunks(cols)

    def step(strip, accs):
        weight = weight_of(strip)
        out = []
        for acc, chunk in zip(accs, chunks):
            part = plan_ref[strip, chunk] * weight
            out.append(acc + jnp.sum(part.reshape(STRIP // 8, 8, LANES), axis=0))
        return tuple(out)

    one, count = strips(rows, step)
    accs = lax.fori_loop(
        0, count, one, tuple(jnp.zeros((8, LANES), F32) for _ in chunks)
    )
    return jnp.concatenate([jnp.sum(a, axis=0, keepdims=True) for a in accs], axis=1)


def first_kernel(n_src, n_tgt, lo_bits, plan, scale, block_s, block_t, *refs):
    pieces, refs = refs[: len(plan)], refs[len(plan) :]
    s_ref, t_ref, a_ref, lse_ref, s_rows, sems, row_tmp = refs
    me_s, me_t = lax.axis_index("src"), lax.axis_index("tgt")
    groups = n_tgt // 2
    copies = []
    for piece, blocks in zip(pieces, plan):
        for index, (kind, source, target) in enumerate(blocks):
            source = me_s ^ pick(source, me_t)
            target = me_t ^ target
            if kind == "s":
                slot = (source >> lo_bits) * groups + (target >> 1)
                place = s_ref.at[:, pl.ds(pl.multiple_of(slot * block_s, block_s), block_s)]
            else:
                slot = (target & 1) * n_src + source
                place = t_ref.at[:, pl.ds(pl.multiple_of(slot * LANES, LANES), LANES)]
            copies.append(pltpu.make_async_copy(piece.at[index], place, sems.at[len(copies)]))
    for copy in copies:
        copy.start()
    for copy in copies:
        copy.wait()
    rows, cols = s_rows.shape[0], t_ref.shape[1]
    s_rows[...] = s_ref[...].T
    chunks = row_chunks(cols)
    wide = 4 * LANES
    bias = jnp.where(real_columns(wide, block_t), 0.0, EMPTY)
    for start in range(0, cols, wide):
        a_ref[:, start : start + wide] = bias + jnp.dot(
            s_rows[...], t_ref[:, start : start + wide], preferred_element_type=F32
        )
    factor = scale * math.log2(math.e)

    def step(strip, carry):
        top = a_ref[strip, chunks[0]]
        for chunk in chunks[1:]:
            top = jnp.maximum(top, a_ref[strip, chunk])
        top = jnp.max(top, axis=1, keepdims=True)
        total = jnp.zeros((STRIP, LANES), F32)
        for chunk in chunks:
            part = jnp.exp2((a_ref[strip, chunk] - top) * factor)
            a_ref[strip, chunk] = part
            total = total + part
        top = top * scale
        a_ref[strip, pl.ds(cols, LANES)] = jnp.broadcast_to(top, (STRIP, LANES))
        row_tmp[strip, :] = top + jnp.log(jnp.sum(total, axis=1, keepdims=True))
        return carry

    one, count = strips(rows, step)
    lax.fori_loop(0, count, one, 0)
    for k in range(rows // LANES):
        part = pl.ds(k * LANES, LANES)
        lse_ref[:, part] = to_lanes(row_tmp[part, :])


def real_columns(cols, block_t):
    return lax.rem(lax.broadcasted_iota(jnp.int32, (1, cols), 1), LANES) < block_t


def pick(masks, me_t):
    even, odd = masks
    return even if even == odd else jnp.where((me_t & 1) == 0, even, odd)


def load_rows(row_ref, tmp_ref):
    for k in range(tmp_ref.shape[0] // LANES):
        part = pl.ds(k * LANES, LANES)
        tmp_ref[part, :] = to_column(row_ref[:, part])


def second_kernel(scale, block_t, s_hbm, t_hbm, a_ref, mine_ref, other_ref, pot_ref, lse_ref, tmp, s_ref, t_ref, sem):
    rows, cols = tmp.shape[0], lse_ref.shape[1]
    pot_ref[...] = -log_add(mine_ref[...], other_ref[...])
    load_rows(pot_ref, tmp)

    def weight(strip):
        return jnp.exp(a_ref[strip, pl.ds(cols, LANES)] + tmp[strip, :])

    sums = jnp.where(real_columns(cols, block_t), column_sums(a_ref, weight, rows, cols), 1.0)
    lse_ref[...] = jnp.log(sums)

    @pl.when(jnp.min(sums) < TINY)
    def _():
        load_both(s_hbm, t_hbm, s_ref, t_ref, sem)
        for start in range(0, cols, LANES):
            logits = jnp.dot(
                s_ref[...].T, t_ref[:, start : start + LANES], preferred_element_type=F32
            )
            logits = logits * scale + tmp[...]
            top = jnp.max(logits, axis=0, keepdims=True)
            total = jnp.sum(jnp.exp(logits - top), axis=0, keepdims=True)
            lse_ref[:, start : start + LANES] = jnp.where(
                real_columns(LANES, block_t), top + jnp.log(total), 0.0
            )


def load_both(s_hbm, t_hbm, s_ref, t_ref, sem):
    first = pltpu.make_async_copy(s_hbm, s_ref, sem.at[0])
    second = pltpu.make_async_copy(t_hbm, t_ref, sem.at[1])
    first.start()
    second.start()
    first.wait()
    second.wait()


def third_kernel(
    scale, block_t, s_hbm, t_hbm, a_in, pot_ref, mine_ref, other_ref, a_ref, lse_ref, cpot_ref, tmp, s_ref, t_ref, sem
):
    del a_in
    rows, cols = tmp.shape[0], mine_ref.shape[1]
    chunks = row_chunks(cols)
    cpot = -log_add(mine_ref[...], other_ref[...])
    high = jnp.max(cpot) > -math.log(TINY)

    @pl.when(high)
    def _():
        load_rows(pot_ref, tmp)
        load_both(s_hbm, t_hbm, s_ref, t_ref, sem)
        for start in range(0, cols, LANES):
            logits = jnp.dot(
                s_ref[...].T, t_ref[:, start : start + LANES], preferred_element_type=F32
            )
            part = logits * scale + tmp[...] + cpot[:, start : start + LANES]
            a_ref[:, start : start + LANES] = jnp.where(
                real_columns(LANES, block_t), jnp.exp(part), 0.0
            )
        a_ref[:, cols : cols + LANES] = jnp.broadcast_to(-tmp[...], (rows, LANES))

    lift = jnp.where(high, 0.0, cpot)
    cpot_ref[...] = cpot - lift
    weight = jnp.exp(lift)

    def step(strip, carry):
        total = jnp.zeros((STRIP, LANES), F32)
        for c, chunk in enumerate(chunks):
            total = total + a_ref[strip, chunk] * weight[:, c * LANES : (c + 1) * LANES]
        total = jnp.sum(total, axis=1, keepdims=True)
        tmp[strip, :] = a_ref[strip, pl.ds(cols, 1)] + jnp.log(total)
        return carry

    one, count = strips(rows, step)
    lax.fori_loop(0, count, one, 0)
    for k in range(rows // LANES):
        part = pl.ds(k * LANES, LANES)
        lse_ref[:, part] = to_lanes(tmp[part, :])


def fourth_kernel(n_tgt, lo_bits, block_t, a_ref, mine_ref, other_ref, pot_ref, own_ref, sum_ref, tmp):
    rows, cols, block_s = tmp.shape[0], sum_ref.shape[1], own_ref.shape[1]
    pot_ref[...] = -log_add(mine_ref[...], other_ref[...])
    slot = (lax.axis_index("src") >> lo_bits) * (n_tgt // 2) + (lax.axis_index("tgt") >> 1)
    own_ref[...] = pot_ref[:, pl.ds(pl.multiple_of(slot * block_s, block_s), block_s)]
    load_rows(pot_ref, tmp)

    def weight(strip):
        return jnp.exp(a_ref[strip, pl.ds(cols, LANES)] + tmp[strip, :])

    sums = column_sums(a_ref, weight, rows, cols)
    sum_ref[...] = jnp.where(real_columns(cols, block_t), sums, 1.0)


def split(x):
    high = x.astype(BF16)
    return high, (x - high.astype(F32)).astype(BF16)


def fifth_kernel(
    n_src, n_tgt, lo_bits, block_s, s_ref, t_ref, a_ref, pot_ref, mine_ref, other_ref, cpot_ref,
    matched_ref, cov_ref, own_ref, tmp, plan, matched, cov, col_tmp
):
    rows, cols, block_t = tmp.shape[0], mine_ref.shape[1], own_ref.shape[1]
    width, half = s_ref.shape[0], cov_ref.shape[1]
    chunks = row_chunks(cols)
    me_s, me_t = lax.axis_index("src"), lax.axis_index("tgt")
    side = me_t & 1
    load_rows(pot_ref, tmp)
    sums = mine_ref[...] + other_ref[...]
    col_tmp[...] = cpot_ref[...] - jnp.log(sums)
    slot = side * n_src + me_s
    own_ref[...] = col_tmp[:, pl.ds(pl.multiple_of(slot * LANES, LANES), LANES)][:, :block_t]
    inverse = 1.0 / sums

    def step(strip, carry):
        weight = jnp.exp(a_ref[strip, pl.ds(cols, LANES)] + tmp[strip, :])
        for c, chunk in enumerate(chunks):
            part = a_ref[strip, chunk] * weight * inverse[:, c * LANES : (c + 1) * LANES]
            plan[strip, chunk] = part.astype(BF16)
        return carry

    one, count = strips(rows, step)
    lax.fori_loop(0, count, one, 0)
    matched[...] = lax.dot_general(t_ref[...], plan[...], NT, preferred_element_type=F32)
    groups = n_tgt // 2
    base = (me_s >> lo_bits) * groups
    for group in range(groups):
        place = base + ((me_t >> 1) ^ group)
        start = pl.multiple_of(place * block_s, block_s)
        matched_ref[group] = matched[:, pl.ds(start, block_s)]
    high, low = split(matched[...])
    cov[...] = jnp.zeros(cov.shape, F32)
    cov[:width, :width] = lax.dot_general(
        s_ref[...], high, NT, preferred_element_type=F32
    ) + lax.dot_general(s_ref[...], low, NT, preferred_element_type=F32)
    for k in range(2):
        cov_ref[k] = cov[pl.ds(pl.multiple_of((side ^ k) * half, 8), half), :]


MAIN = 256
TAIL = 64


def tails(high, low, other):
    return (high + pltpu.roll(other, TAIL, 1)).astype(BF16), low.astype(BF16)


def polar_kernel(s_ref, mine_ref, other_ref, ortho_ref, rotated_ref, x_ref, high, low, left, right, below, gram_high, gram_low, gram_tail):
    width, half = ortho_ref.shape[0], mine_ref.shape[0]
    rows = 2 * half
    tail = rows - MAIN
    side = lax.axis_index("tgt") & 1
    x_ref[pl.ds(pl.multiple_of(side * half, 8), half), :] = mine_ref[...]
    x_ref[pl.ds(pl.multiple_of((1 - side) * half, 8), half), :] = other_ref[...]
    cov = x_ref[...]
    x_ref[...] = cov / jnp.sqrt(jnp.sum(cov * cov) + 1e-06)
    below[...] = jnp.zeros(below.shape, BF16)

    def beside(*parts):
        return jnp.concatenate(parts, axis=1)

    def left_of(part):
        return beside(high[part, :MAIN], high[part, :MAIN], low[part, :MAIN], left[part, :])

    def right_of(part):
        return beside(high[part, :MAIN], low[part, :MAIN], high[part, :MAIN], right[part, :])

    def step(index, carry):
        x = x_ref[...]
        x_high = x.astype(BF16)
        rest = x - x_high.astype(F32)
        x_low = rest.astype(BF16)
        high[...] = x_high
        low[...] = x_low
        high_tail, low_tail = x_high[:, MAIN:].astype(F32), rest[:, MAIN:]
        left[:, :LANES], left[:, LANES:] = tails(high_tail, low_tail, high_tail)
        right[:, :LANES], right[:, LANES:] = tails(high_tail, high_tail, low_tail)
        for k, part in enumerate((x_high, x_low, x_high)):
            below[k * TAIL : k * TAIL + tail, :] = part[MAIN:]
        first, last = slice(0, MAIN), slice(MAIN, rows)
        gram = lax.dot_general(
            left_of(slice(0, rows)), right_of(first), NT, preferred_element_type=F32
        )
        corner = lax.dot_general(left_of(last), right_of(last), NT, preferred_element_type=F32)
        corner = jnp.concatenate([gram[MAIN:, :].T, corner], axis=0)
        corner = beside(corner, jnp.zeros((rows, LANES - tail), F32))
        part = gram.astype(BF16)
        gram_high[...] = part
        gram_low[...] = (gram - part.astype(F32)).astype(BF16)
        corner_high = corner.astype(BF16).astype(F32)
        gram_tail[:, :LANES], gram_tail[:, LANES:] = tails(
            corner_high, corner - corner_high, corner_high
        )
        product = jnp.dot(
            beside(gram_high[...], gram_high[...], gram_low[...], gram_tail[...]),
            jnp.concatenate(
                [high[:MAIN, :rows], low[:MAIN, :rows], high[:MAIN, :rows], below[:, :rows]], axis=0
            ),
            preferred_element_type=F32,
        )
        x_ref[:, :rows] = 1.5 * x_ref[:, :rows] - 0.5 * product
        return carry

    lax.fori_loop(0, NEWTON, step, 0)
    ortho = x_ref[:width, :width]
    ortho_ref[...] = ortho
    ortho_high, ortho_low = split(ortho)
    rotated = lax.dot_general(
        ortho_high, s_ref[...], TN, preferred_element_type=F32
    ) + lax.dot_general(ortho_low, s_ref[...], TN, preferred_element_type=F32)
    rotated_ref[...] = rotated.astype(BF16)


def log2(n):
    return n.bit_length() - 1


def make_body(n_src, n_tgt):
    groups = n_tgt // 2

    def send(x, masks):
        pairs = []
        for s in range(n_src):
            for t in range(n_tgt):
                source, target = masks[t & 1]
                pairs.append((s * n_tgt + t, (s ^ source) * n_tgt + (t ^ target)))
        return lax.ppermute(x, ("src", "tgt"), pairs)

    def shifted(blocks, masks, crossed=False):
        out = []
        for kind, source, target in blocks:
            source = source[::-1] if crossed else source
            source = tuple(a ^ m[0] for a, m in zip(source, masks))
            out.append((kind, source, target ^ masks[0][1]))
        return out

    def groups_of(parts):
        return [parts] if len(parts) < 2 else [parts[:-1], parts[-1:]]

    def send_parts(parts, masks, crossed=False):
        out = []
        for group in groups_of(parts):
            whole = jnp.concatenate([x for x, _ in group], axis=0) if len(group) > 1 else group[0][0]
            blocks = [block for _, names in group for block in names]
            out.append((send(whole, masks), shifted(blocks, masks, crossed)))
        return out

    def gather(source_t, target_t, high_src, low_src, high_tgt):
        pad = ((0, 0), (0, source_t.shape[1] - target_t.shape[1]))
        both = lax.optimization_barrier(jnp.stack([source_t, jnp.pad(target_t, pad)]))
        pairs = [(both, [("s", (0, 0), 0), ("t", (0, 0), 0)])]
        for mask in high_src[::-1]:
            masks = (mask, mask)
            pairs += [(send(x, masks), shifted(blocks, masks)) for x, blocks in pairs]
        sources = [(x[:1], blocks[:1]) for x, blocks in pairs]
        targets = [(x[1:], blocks[1:]) for x, blocks in pairs]
        parts = list(pairs)
        core = ((0, 1), (0, 1))
        parts += send_parts(targets, core, True)
        for k in range(max(len(high_tgt), len(low_src))):
            if k < len(low_src):
                more = send_parts(targets, (low_src[k], low_src[k]))
                targets = targets + more
                parts += more
                for part in more:
                    parts += send_parts([part], core, True)
            if k < len(high_tgt):
                more = send_parts(sources, (high_tgt[k], high_tgt[k]))
                sources = sources + more
                parts += more
        return [x for x, _ in parts], [blocks for _, blocks in parts]

    def meet(x, stages, combine):
        for mask in stages[:-1]:
            x = combine(x, send(x, (mask, mask)))
        return x, send(x, (stages[-1], stages[-1]))

    def body(source_words, target_words):
        block_s, width = source_words.shape
        block_t = target_words.shape[0]
        scale = 4.0 / math.sqrt(width)
        assert block_t <= LANES
        cols = LANES * n_src * 2
        rep = n_src
        while rep > 1 and block_s * rep * groups * cols * 4 > 9 * 2**20:
            rep //= 2
        rows = block_s * rep * groups
        lo_bits = log2(n_src // rep)
        bits = log2(n_src)
        low_src = [(1 << k, 0) for k in range(lo_bits)]
        high_src = [(1 << k, 0) for k in range(lo_bits, bits)]
        high_tgt = [(0, 1 << k) for k in range(1, log2(n_tgt))]
        core = [(0, 1)]
        source_t = source_words.T
        pieces, plan = gather(source_t, target_words.T, high_src, low_src, high_tgt)

        shape = jax.ShapeDtypeStruct
        a_shape = shape((rows, cols + LANES), F32)
        row_shape, col_shape = shape((1, rows), F32), shape((1, cols), F32)
        s_shape, t_shape = shape((width, rows), BF16), shape((width, cols), BF16)
        big = rows * cols * 4 > 9 * 2**20
        params = pltpu.CompilerParams(vmem_limit_bytes=(56 if big else 16) * 2**20)
        tmp = pltpu.VMEM((rows, 1), F32)
        again = [pltpu.VMEM(s_shape.shape, BF16), pltpu.VMEM(t_shape.shape, BF16), pltpu.SemaphoreType.DMA((2,))]

        s_all, t_all, block, row_lse = pl.pallas_call(
            functools.partial(first_kernel, n_src, n_tgt, lo_bits, plan, scale, block_s, block_t),
            out_shape=(s_shape, t_shape, a_shape, row_shape),
            in_specs=[ANY] * len(pieces),
            out_specs=(VMEM,) * 4,
            scratch_shapes=[
                pltpu.VMEM((rows, width), BF16),
                pltpu.SemaphoreType.DMA((rows // block_s + cols // LANES,)),
                tmp,
            ],
            compiler_params=params,
        )(*pieces)

        mine, other = meet(row_lse, high_tgt, log_add)
        row_pot, col_lse = pl.pallas_call(
            functools.partial(second_kernel, scale, block_t),
            out_shape=(row_shape, col_shape),
            in_specs=[ANY, ANY, VMEM, VMEM, VMEM],
            out_specs=(VMEM,) * 2,
            scratch_shapes=[tmp] + again,
            compiler_params=params,
        )(s_all, t_all, block, mine, other)

        mine, other = meet(col_lse, core + low_src, log_add)
        block, row_lse, col_base = pl.pallas_call(
            functools.partial(third_kernel, scale, block_t),
            out_shape=(a_shape, row_shape, col_shape),
            in_specs=[ANY, ANY, VMEM, VMEM, VMEM, VMEM],
            out_specs=(VMEM,) * 3,
            input_output_aliases={2: 0},
            scratch_shapes=[tmp] + again,
            compiler_params=params,
        )(s_all, t_all, block, row_pot, mine, other)

        mine, other = meet(row_lse, high_tgt, log_add)
        row_pot, row_part, col_sum = pl.pallas_call(
            functools.partial(fourth_kernel, n_tgt, lo_bits, block_t),
            out_shape=(row_shape, shape((1, block_s), F32), col_shape),
            in_specs=[VMEM] * 3,
            out_specs=(VMEM,) * 3,
            scratch_shapes=[tmp],
            compiler_params=params,
        )(block, mine, other)

        mine, other = meet(col_sum, core + low_src, jnp.add)
        assert 0 < width - MAIN <= TAIL
        half = (width + 15) // 16 * 8
        padded = (width + LANES - 1) // LANES * LANES
        matched, cov, col_part = pl.pallas_call(
            functools.partial(fifth_kernel, n_src, n_tgt, lo_bits, block_s),
            out_shape=(
                shape((groups, width, block_s), F32),
                shape((2, half, padded), F32),
                shape((1, block_t), F32),
            ),
            in_specs=[VMEM] * 7,
            out_specs=(VMEM,) * 3,
            scratch_shapes=[
                tmp,
                pltpu.VMEM((rows, cols), BF16),
                pltpu.VMEM((width, rows), F32),
                pltpu.VMEM((2 * half, padded), F32),
                pltpu.VMEM((1, cols), F32),
            ],
            compiler_params=params,
        )(s_all, t_all, block, row_pot, mine, other, col_base)

        part = cov[0] + send(cov[1], (core[0], core[0]))
        stages = low_src + high_tgt
        for k in range(len(stages)):
            part = part + send(part, (stages[k], stages[(k + 1) % len(stages)]))
        own_matched = matched[0]
        rest = send(part, (core[0], core[0]))
        late = [send(matched[k], ((0, 2 * k), (0, 2 * k))) for k in range(1, groups)]

        ortho, rotated = pl.pallas_call(
            polar_kernel,
            out_shape=(shape((width, width), F32), shape((width, block_s), BF16)),
            in_specs=[VMEM] * 3,
            out_specs=(VMEM,) * 2,
            scratch_shapes=[
                pltpu.VMEM((2 * half, padded), F32),
                pltpu.VMEM((2 * half, padded), BF16),
                pltpu.VMEM((2 * half, padded), BF16),
                pltpu.VMEM((2 * half, 2 * LANES), BF16),
                pltpu.VMEM((2 * half, 2 * LANES), BF16),
                pltpu.VMEM((4 * TAIL, padded), BF16),
                pltpu.VMEM((2 * half, MAIN), BF16),
                pltpu.VMEM((2 * half, MAIN), BF16),
                pltpu.VMEM((2 * half, 2 * LANES), BF16),
            ],
            compiler_params=params,
        )(source_t, part, rest)
        own_matched, rotated = lax.optimization_barrier((own_matched, rotated))
        for theirs in late:
            own_matched = own_matched + theirs
        return (rotated.T, own_matched.T, ortho, row_part[0], col_part[0])

    return body


def solution(mesh):
    in_specs = (P(("src", "tgt"), None), P(("tgt", "src"), None))
    out_specs = (
        P(("src", "tgt"), None),
        P(("src", "tgt"), None),
        P(),
        P(("src", "tgt")),
        P(("tgt", "src")),
    )
    body = make_body(mesh.shape["src"], mesh.shape["tgt"])
    return jax.shard_map(body, mesh=mesh, in_specs=in_specs, out_specs=out_specs, check_vma=False)
```
